256 devices in a mesh: leaf: 16 (over y, x), panel: 16 (over z, core).
Axes of the slice: x: 4, y: 4, z: 8, core: 2. Of those that a mesh axis runs over, the one named last changes fastest.
Arguments:
- right_sides: bfloat16 [3, 49152, 128], P(None, ('leaf', 'panel')), may hold values from -6 to 6
- inverse_low: bfloat16 [49152, 3072], P(('leaf', 'panel')), may hold values from -1 to 1, as said below
- inverse_mid: bfloat16 [49152, 6144], P(('leaf', 'panel')), may hold values from -1 to 1, as said below
- inverse_top: bfloat16 [49152, 12288], P(('leaf', 'panel')), may hold values from -1 to 1, as said below
- update_low: bfloat16 [49152, 3072], P(('leaf', 'panel')), may hold values from -0.109375 to 0.109375
- update_mid: bfloat16 [49152, 6144], P(('leaf', 'panel')), may hold values from -0.078125 to 0.078125
- slots_low: int32 [16, 3072], replicated, may hold values from 0 to 6143, as said below
- slots_mid: int32 [8, 6144], replicated, may hold values from 0 to 12287, as said below
Outputs:
- solutions: bfloat16 [3, 49152, 128], P(None, ('leaf', 'panel'))
The draws below stay inside these ranges and needn't reach their ends.
Inputs may be any that keep to these rules, and one draw needn't show every extreme that they name: `inverse_low`: within each supernode's rows, the block is lower triangular with a unit diagonal. `inverse_mid`: within each supernode's rows, the block is lower triangular with a unit diagonal. `inverse_top`: within each supernode's rows, the block is lower triangular with a unit diagonal. `slots_low`: each row lists 3072 distinct rows of the parent supernode. `slots_mid`: each row lists 6144 distinct rows of the parent supernode.
All inputs are finite; a program needn't handle non-finite values.
Results may differ from the reference program's by a relative error of at most 0.015.
Values may be sent and summed in bfloat16 or wider, within the bound.
A program may use at most 128 MiB of HBM per device.

```python
import math
import jax
import jax.numpy as jnp
from jax import lax

SEP0 = 3072
VEC = 128
LEVELS = 3
SEP1 = 6144
SEP2 = 12288
ROWS = 49152
NODES = 16
PAIRS = 8


def lower_inverse(key, extent):
    row_at = lax.broadcasted_iota(jnp.int32, (ROWS, extent), 0) % extent
    col_at = lax.broadcasted_iota(jnp.int32, (ROWS, extent), 1)
    random_part = jnp.clip(jax.random.normal(key, (ROWS, extent), jnp.float32), -6.0, 6.0)
    lower_part = jnp.where(col_at < row_at, random_part * (1.0 / math.sqrt(extent)), 0.0)
    return (lower_part + jnp.where(col_at == row_at, 1.0, 0.0)).astype(jnp.bfloat16)


def draw_inverse_low(key, part):
    return lower_inverse(key, SEP0)


def draw_inverse_mid(key, part):
    return lower_inverse(key, SEP1)


def draw_inverse_top(key, part):
    return lower_inverse(key, SEP2)


def parent_slots(key, number, listed, extent):

    def single(subkey):
        first_key, second_key = jax.random.split(subkey)
        middle = 1 + jax.random.permutation(first_key, extent - 2)[:listed - 2]
        chosen = jnp.concatenate([jnp.array([0, extent - 1], jnp.int32), middle.astype(jnp.int32)])
        return jax.random.permutation(second_key, chosen)
    return jax.vmap(single)(jax.random.split(key, number))


def draw_slots_low(key, part):
    return parent_slots(key, NODES, SEP0, SEP1)


def draw_slots_mid(key, part):
    return parent_slots(key, PAIRS, SEP1, SEP2)


def steps_of(stream_key, dims, cuts, least, high):
    def one(dim, parts):
        heights = jax.random.uniform(jax.random.fold_in(jax.random.fold_in(stream_key, 6), dim), (parts,), jnp.float32, least / len(cuts), high / len(cuts))
        return jnp.repeat(jnp.exp(heights), dims[dim] // parts).reshape((-1,) + (1,) * (len(dims) - dim - 1))

    gain = one(*cuts[0])
    for cut in cuts[1:]:
        gain = gain * one(*cut)
    return gain


def normal_values(stream_key, dims, deviation, reach, shards=(), kind=jnp.bfloat16):
    result = deviation * jax.random.normal(stream_key, dims, jnp.float32)
    if shards:
        result = result * steps_of(stream_key, dims, shards, -0.22, 0.18)
    return jnp.clip(result, -reach, reach).astype(kind)


def setup_inputs(seed: int = 0) -> dict:
    key_of = jax.random.split(jax.random.key(seed), 9)
    return {
        "right_sides": normal_values(key_of[0], (LEVELS, ROWS, VEC), 1.0, 6.0, ((1, 256),)),
        "inverse_low": draw_inverse_low(jax.random.fold_in(key_of[8], 71), 0),
        "inverse_mid": draw_inverse_mid(jax.random.fold_in(key_of[8], 71), 0),
        "inverse_top": draw_inverse_top(jax.random.fold_in(key_of[8], 71), 0),
        "update_low": normal_values(key_of[4], (ROWS, SEP0), SEP0 ** -0.5, 0.109375, ((0, 256),)),
        "update_mid": normal_values(key_of[5], (ROWS, SEP1), SEP1 ** -0.5, 0.078125, ((0, 256),)),
        "slots_low": draw_slots_low(jax.random.fold_in(key_of[8], 71), 0),
        "slots_mid": draw_slots_mid(jax.random.fold_in(key_of[8], 71), 0),
    }


def reference(right_sides, inverse_low, inverse_mid, inverse_top, update_low, update_mid, slots_low, slots_mid):
    inverses = (inverse_low, inverse_mid, inverse_top)
    updates = (update_low, update_mid)
    lists = (slots_low, slots_mid)
    solved = []
    targets_all = []
    carried = None
    for height_at in range(LEVELS):
        extent = SEP0 * 2 ** height_at
        node_count = ROWS // extent
        if height_at == 0:
            local_rows = right_sides[0]
        else:
            local_rows = (right_sides[height_at].astype(jnp.float32) - carried).astype(jnp.bfloat16)
        blocks = local_rows.reshape(node_count, extent, VEC)
        matrices = inverses[height_at].reshape(node_count, extent, extent)
        solved_now = lax.map(lambda operands: jnp.dot(operands[0], operands[1], preferred_element_type=jnp.float32), (matrices, blocks)).astype(jnp.bfloat16)
        solved.append(solved_now)
        if height_at + 1 < LEVELS:
            update_mats = updates[height_at].reshape(node_count, extent, extent)
            products = lax.map(lambda operands: lax.dot_general(operands[0], operands[1], (((0,), (0,)), ((), ())), preferred_element_type=jnp.float32), (update_mats, solved_now))
            parents = (jnp.arange(node_count, dtype=jnp.int32) // 2) * (2 * extent)
            targets = (lists[height_at].astype(jnp.int32) + parents[:, None]).reshape(-1)
            targets_all.append(targets)
            carried = jax.ops.segment_sum(products.reshape(-1, VEC), targets, num_segments=ROWS)
    results = [None] * LEVELS
    above = None
    for height_at in reversed(range(LEVELS)):
        extent = SEP0 * 2 ** height_at
        node_count = ROWS // extent
        matrices = inverses[height_at].reshape(node_count, extent, extent)
        solved_now = solved[height_at]
        if height_at + 1 < LEVELS:
            update_mats = updates[height_at].reshape(node_count, extent, extent)
            picked = jnp.take(above, targets_all[height_at], axis=0).reshape(node_count, extent, VEC)
            correction = lax.map(lambda operands: jnp.dot(operands[0], operands[1], preferred_element_type=jnp.float32), (update_mats, picked))
            target = (solved_now.astype(jnp.float32) - correction).astype(jnp.bfloat16)
        else:
            target = solved_now
        result_now = lax.map(lambda operands: lax.dot_general(operands[0], operands[1], (((0,), (0,)), ((), ())), preferred_element_type=jnp.float32), (matrices, target))
        above = result_now.astype(jnp.bfloat16).reshape(ROWS, VEC)
        results[height_at] = above
    return jnp.stack(results)
```

```python
import functools

import jax
import jax.numpy as jnp
from jax import lax
from jax.experimental import pallas as pl
from jax.experimental.pallas import tpu as pltpu
from jax.sharding import PartitionSpec as P

BF = jnp.bfloat16
F32 = jnp.float32
ROWS = 192
HALF = 96
VEC = 128
RING = 8
CORES = 2
SLAB = ROWS * CORES
STEP = 2 * SLAB
PANELS = RING * CORES
GATHERS = (1, 1, 2, 2, 4, 2, 1)
REDUCES = (1, 2, 4, 2, 2, 1, 1)
DATA_SEMS = 400


class Sems:
    def __init__(self, send, recv):
        self.send, self.recv, self.at = send, recv, 0

    def take(self):
        at = self.at
        self.at += 1
        return self.send.at[at], self.recv.at[at]


def kernel(
    rs, il, im, it, ul, um, sl, sm, out,
    wl, wm, wt, vl, vm, pick0, pick1, part,
    ag0, ag1, ag2, ag3, ag4, ag5, ag6,
    dr0, dr1, dr2, dr3, dr4, dr5, dr6,
    rp0, rp1, rp2, rp3, rp4, rp5, rp6,
    xr0, xr1, xr2, xr3, xr4, xr5, xr6,
    dsend, rsend, xsend, esend, erecv, pair_rows, solved,
    wsem, send_sem, recv_sem,
):
    gathers = (ag0, ag1, ag2, ag3, ag4, ag5, ag6)
    core_in = (dr0, dr1, dr2, dr3, dr4, dr5, dr6)
    ring_in = (rp0, rp1, rp2, rp3, rp4, rp5, rp6)
    leaf_in = (xr0, xr1, xr2, xr3, xr4, xr5, xr6)
    leaf = lax.axis_index("leaf")
    panel = lax.axis_index("panel")
    z = panel // 2
    c = panel % 2
    x = leaf % 4
    base = leaf - x

    def zmod(v):
        return (v + 2 * RING) % RING

    up = (leaf, zmod(z + 1) * 2 + c)
    down = (leaf, zmod(z - 1) * 2 + c)
    core = (leaf, z * 2 + 1 - c)

    def flip(v, d):
        if d == 1:
            return v + 1 - 2 * (v % 2)
        if d == 2:
            return (v + 2) % 4
        return 3 - v

    def leaf_peer(d):
        return (base + flip(x, d), panel)

    sems = Sems(send_sem, recv_sem)

    def remote(src, dst, device):
        send, recv = sems.take()
        copy = pltpu.make_async_remote_copy(
            src_ref=src, dst_ref=dst, send_sem=send, recv_sem=recv,
            device_id=device, device_id_type=pl.DeviceIdType.MESH,
        )
        copy.start()
        return copy

    loads = []
    for at, (src, dst) in enumerate(((il, wl), (ul, vl), (im, wm), (um, vm), (it, wt))):
        copy = pltpu.make_async_copy(src, dst, wsem.at[at])
        copy.start()
        loads.append(copy)

    barrier = pltpu.get_barrier_semaphore()
    for device in (up, down, core, leaf_peer(1), leaf_peer(2), leaf_peer(3)):
        pl.semaphore_signal(barrier, inc=1, device_id=device, device_id_type=pl.DeviceIdType.MESH)
    pl.semaphore_wait(barrier, 6)

    gather_at = [0]
    reduce_at = [0]
    swap_at = [0]

    def all_gather(nx, value, beside=None):
        buf = gathers[gather_at[0]]
        gather_at[0] += 1
        xi = x % nx
        buf[xi, z, c] = value
        sends = []
        if nx > 1:
            mine = buf.at[xi, z, c]
            for d in range(1, nx):
                sends.append(remote(mine, mine, leaf_peer(d)))
            for copy in sends:
                copy.wait_recv()
        own = buf.at[:, z, c]
        plus = remote(own, own, up)
        minus = remote(own, own, down)
        cores = [remote(own, own, core)]
        sends += [plus, minus]
        if beside is not None:
            beside()
        for s in range(1, 4):
            lower = buf.at[:, zmod(z - s), c]
            upper = buf.at[:, zmod(z + s), c]
            plus.wait_recv()
            if s < 3:
                nplus = remote(lower, lower, up)
            else:
                half = buf.at[:, zmod(z - s), c, pl.ds(0, HALF)]
                nplus = remote(half, half, up)
            cores.append(remote(lower, lower, core))
            minus.wait_recv()
            if s < 3:
                nminus = remote(upper, upper, down)
            else:
                half = buf.at[:, zmod(z + s), c, pl.ds(HALF, HALF)]
                nminus = remote(half, half, down)
            cores.append(remote(upper, upper, core))
            plus, minus = nplus, nminus
            sends += [plus, minus]
        plus.wait_recv()
        minus.wait_recv()
        far = buf.at[:, zmod(z + 4), c]
        cores.append(remote(far, far, core))
        for copy in cores:
            copy.wait_recv()
        for copy in sends + cores:
            copy.wait_send()
        return buf

    def reduce_scatter(nx):
        at = reduce_at[0]
        reduce_at[0] += 1
        cin, rin, lin = core_in[at], ring_in[at], leaf_in[at]
        order = (4, 3, -3, 2, -2, 1, -1, 0)
        cores = {}
        for off in order:
            zz = zmod(z + off)
            for xi in range(nx):
                dsend[xi, zz] = part[xi * PANELS + 2 * zz + 1 - c].astype(BF)
            piece = dsend.at[pl.ds(0, nx), zz]
            cores[off] = remote(piece, cin.at[:, zz], core)

        def total(off):
            zz = zmod(z + off)
            cores[off].wait_recv()
            return [part[xi * PANELS + 2 * zz + c] + cin[xi, zz].astype(F32) for xi in range(nx)]

        def half_added(values, ref, low):
            done = []
            for xi in range(nx):
                if low:
                    done.append(jnp.concatenate(
                        [values[xi][:HALF] + ref[xi, :HALF].astype(F32), values[xi][HALF:]], 0))
                else:
                    done.append(jnp.concatenate(
                        [values[xi][:HALF], values[xi][HALF:] + ref[xi, HALF:].astype(F32)], 0))
            return done

        def put(slot, values):
            for xi in range(nx):
                rsend[slot, xi] = values[xi].astype(BF)

        sends = []
        put(0, total(4))
        lo, hi = pl.ds(0, HALF), pl.ds(HALF, HALF)
        g = pl.ds(0, nx)
        plus = remote(rsend.at[0, g, lo], rin.at[0, 0, :, lo], up)
        minus = remote(rsend.at[0, g, hi], rin.at[1, 0, :, hi], down)
        sends += [plus, minus]
        for s in range(1, 4):
            for sign in (0, 1):
                off = (4 - s) if sign == 0 else s - 4
                values = total(off)
                (plus, minus)[sign].wait_recv()
                got = rin.at[sign, s - 1]
                if s == 1:
                    values = half_added(values, got, sign == 0)
                else:
                    values = [values[xi] + got[xi].astype(F32) for xi in range(nx)]
                slot = 2 * s - 1 + sign
                put(slot, values)
                nxt = remote(rsend.at[slot, g], rin.at[sign, s], (up, down)[sign])
                sends.append(nxt)
                if sign == 0:
                    plus = nxt
                else:
                    minus = nxt
        values = total(0)
        plus.wait_recv()
        minus.wait_recv()
        values = [
            values[xi] + rin[0, 3, xi].astype(F32) + rin[1, 3, xi].astype(F32) for xi in range(nx)
        ]
        if nx == 1:
            result = values[0]
        else:
            for xi in range(nx):
                xsend[xi] = values[xi]
            moves = []
            for d in range(1, nx):
                esend[d] = xsend[flip(x, d) % nx].astype(BF)
                moves.append(remote(esend.at[d], lin.at[d], leaf_peer(d)))
            result = xsend[x % nx]
            for d in range(1, nx):
                moves[d - 1].wait_recv()
                result = result + lin[d].astype(F32)
            sends += moves
        for copy in sends + list(cores.values()):
            copy.wait_send()
        return result

    def swap(value, d):
        at = swap_at[0]
        swap_at[0] += 1
        esend[0] = value
        copy = remote(esend.at[0], erecv.at[at], leaf_peer(d))
        copy.wait_recv()
        got = erecv[at]
        copy.wait_send()
        return got

    def apply(weight, buf, nx, rows):
        def body(i, acc):
            lanes = pl.ds(pl.multiple_of(i * STEP, STEP), STEP)
            block = buf[i // 4, pl.ds((i % 4) * 2, 2)].reshape(STEP, VEC)
            return acc + jnp.dot(weight[:, lanes], block, preferred_element_type=F32)

        return lax.fori_loop(0, 4 * nx, body, jnp.zeros((rows, VEC), F32))

    def apply_t(weight, value, nx):
        def body(i, carry):
            lanes = pl.ds(pl.multiple_of(i * STEP, STEP), STEP)
            got = lax.dot_general(
                weight[:, lanes], value, (((0,), (0,)), ((), ())), preferred_element_type=F32
            )
            part[pl.ds(4 * i, 4)] = got.reshape(4, ROWS, VEC)
            return carry

        lax.fori_loop(0, 4 * nx, body, 0)

    def build_pick(pick, lists, row, nx, distance):
        here = (x % (2 * nx)) * (PANELS * ROWS) + panel * ROWS
        there = (flip(x, distance) % (2 * nx)) * (PANELS * ROWS) + panel * ROWS

        def body(i, carry):
            lanes = pl.ds(pl.multiple_of(i * SLAB, SLAB), SLAB)
            listed = lists[pl.ds(row, 1), lanes]
            at = lax.broadcasted_iota(jnp.int32, (ROWS, SLAB), 0)
            pick[pl.ds(0, ROWS), lanes] = jnp.where(at == listed - here, 1.0, 0.0).astype(BF)
            pick[pl.ds(ROWS, ROWS), lanes] = jnp.where(at == listed - there, 1.0, 0.0).astype(BF)
            return carry

        lax.fori_loop(0, 8 * nx, body, 0)

    def build_picks():
        build_pick(pick0, sl, leaf, 1, 1)
        build_pick(pick1, sm, leaf // 2, 2, 2)

    picks = (pick0, pick1)
    widths = (1, 2, 4)
    weights = (wl, wm, wt)
    updates = (vl, vm)
    load_of = {"w": (0, 2, 4), "v": (1, 3)}
    rhs = rs[0]
    for level in range(3):
        nx = widths[level]
        buf = all_gather(nx, rhs, build_picks if level == 0 else None)
        loads[load_of["w"][level]].wait()
        y = apply(weights[level], buf, nx, ROWS).astype(BF)
        solved[level] = y
        if level < 2:
            loads[load_of["v"][level]].wait()
            apply_t(updates[level], y, nx)
            mine = reduce_scatter(nx).astype(BF)
            buf = all_gather(nx, mine)
            chosen = apply(picks[level], buf, nx, SLAB)
            other = swap(chosen[ROWS:].astype(BF), nx)
            carried = chosen[:ROWS] + other.astype(F32)
            rhs = (rs[level + 1].astype(F32) - carried).astype(BF)
    target = solved[2]
    for level in (2, 1, 0):
        nx = widths[level]
        if level < 2:
            other = swap(above, nx)
            pair_rows[pl.ds(0, ROWS)] = above
            pair_rows[pl.ds(ROWS, ROWS)] = other
            apply_t(picks[level], pair_rows[...], nx)
            mine = reduce_scatter(nx).astype(BF)
            buf = all_gather(nx, mine)
            correction = apply(updates[level], buf, nx, ROWS)
            target = (solved[level].astype(F32) - correction).astype(BF)
        apply_t(weights[level], target, nx)
        above = reduce_scatter(nx).astype(BF)
        out[level] = above


def on_device(*args):
    vmem = pl.BlockSpec(memory_space=pltpu.VMEM)
    hbm = pl.BlockSpec(memory_space=pl.ANY)
    scratch = [
        pltpu.VMEM((ROWS, 3072), BF),
        pltpu.VMEM((ROWS, 6144), BF),
        pltpu.VMEM((ROWS, 12288), BF),
        pltpu.VMEM((ROWS, 3072), BF),
        pltpu.VMEM((ROWS, 6144), BF),
        pltpu.VMEM((SLAB, 3072), BF),
        pltpu.VMEM((SLAB, 6144), BF),
        pltpu.VMEM((4 * PANELS, ROWS, VEC), F32),
    ]
    scratch += [pltpu.VMEM((nx, RING, CORES, ROWS, VEC), BF) for nx in GATHERS]
    scratch += [pltpu.VMEM((nx, RING, ROWS, VEC), BF) for nx in REDUCES]
    scratch += [pltpu.VMEM((2, 4, nx, ROWS, VEC), BF) for nx in REDUCES]
    scratch += [pltpu.VMEM((nx, ROWS, VEC), BF) for nx in REDUCES]
    scratch += [
        pltpu.VMEM((4, RING, ROWS, VEC), BF),
        pltpu.VMEM((7, 4, ROWS, VEC), BF),
        pltpu.VMEM((4, ROWS, VEC), F32),
        pltpu.VMEM((4, ROWS, VEC), BF),
        pltpu.VMEM((4, ROWS, VEC), BF),
        pltpu.VMEM((SLAB, VEC), BF),
        pltpu.VMEM((3, ROWS, VEC), BF),
        pltpu.SemaphoreType.DMA((5,)),
        pltpu.SemaphoreType.DMA((DATA_SEMS,)),
        pltpu.SemaphoreType.DMA((DATA_SEMS,)),
    ]
    return pl.pallas_call(
        kernel,
        out_shape=jax.ShapeDtypeStruct((3, ROWS, VEC), BF),
        in_specs=[vmem, hbm, hbm, hbm, hbm, hbm, vmem, vmem],
        out_specs=vmem,
        scratch_shapes=scratch,
        compiler_params=pltpu.CompilerParams(
            collective_id=0, has_side_effects=True, vmem_limit_bytes=60 * 1024 * 1024
        ),
    )(*args)


def solution(mesh):
    split = P(("leaf", "panel"), None)
    return jax.shard_map(
        on_device,
        mesh=mesh,
        in_specs=(
            P(None, ("leaf", "panel"), None), split, split, split, split, split, P(), P(),
        ),
        out_specs=P(None, ("leaf", "panel"), None),
        check_vma=False,
    )
```

```python
import jax
import jax.numpy as jnp
from jax import lax
from jax.experimental import pallas as pl
from jax.experimental.pallas import tpu as pltpu
from jax.sharding import PartitionSpec as P

BF = jnp.bfloat16
F32 = jnp.float32
ROWS = 192
VEC = 128
RING = 8
CORES = 2
SLAB = ROWS * CORES
COLS = RING * SLAB
PHASES = 7
EXCHANGES = 8
PER_PHASE = 15
BULK_AT = 2 * PHASES * PER_PHASE + EXCHANGES * 3
DATA_SEMS = BULK_AT + 8
MESH = pl.DeviceIdType.MESH


def kernel(
    rs, il, im, it, ul, um, sl, sm, out,
    w0, w1, w2, v0, v1, pick0, pick1, part, acc, gathers, core_in, ring_in, leaf_in,
    dsend, rsend, esend, vals, solved, wsem, send_sem, recv_sem,
):
    leaf = lax.axis_index("leaf")
    panel = lax.axis_index("panel")
    z = panel // 2
    c = panel % 2
    x = leaf % 4
    xi = leaf % 2
    base = leaf - x

    def ring(off):
        return (z + off + RING) % RING

    def chip(off):
        return (leaf, ring(off) * 2 + c)

    core = (leaf, z * 2 + 1 - c)

    def flip(d):
        if d == 1:
            return x + 1 - 2 * xi
        if d == 2:
            return (x + 2) % 4
        return 3 - x

    def peer(d):
        return (base + flip(d), panel)

    def far_first(k):
        return jnp.where(k % 2 == 1, 4 + (k + 1) // 2, 4 - k // 2)

    def remote(at, src, dst, device):
        return pltpu.make_async_remote_copy(
            src_ref=src, dst_ref=dst, send_sem=send_sem.at[at], recv_sem=recv_sem.at[at],
            device_id=device, device_id_type=MESH,
        )

    def columns(block):
        return pl.ds(pl.multiple_of(block * COLS, COLS), COLS)

    def lanes(zz):
        return pl.ds(pl.multiple_of(zz * SLAB, SLAB), SLAB)

    mine = [
        pltpu.make_async_copy(il, w0.at[0], wsem.at[0]),
        pltpu.make_async_copy(ul, v0.at[0], wsem.at[1]),
        pltpu.make_async_copy(im.at[:, columns(xi)], w1.at[xi], wsem.at[2]),
        pltpu.make_async_copy(um.at[:, columns(xi)], v1.at[xi], wsem.at[3]),
        pltpu.make_async_copy(it.at[:, columns(x)], w2.at[x], wsem.at[4]),
    ]
    for copy in mine:
        copy.start()

    peers = [chip(off) for off in range(1, RING)] + [core] + [peer(d) for d in (1, 2, 3)]
    barrier = pltpu.get_barrier_semaphore()
    for device in peers:
        pl.semaphore_signal(barrier, inc=1, device_id=device, device_id_type=MESH)
    pl.semaphore_wait(barrier, len(peers))

    bulk_w1 = [remote(BULK_AT, im.at[:, columns(1 - xi)], w1.at[xi], peer(1))]
    bulk_v1 = [remote(BULK_AT + 1, um.at[:, columns(1 - xi)], v1.at[xi], peer(1))]
    bulk_w2 = [
        remote(BULK_AT + 1 + d, it.at[:, columns(flip(d))], w2.at[x], peer(d)) for d in (1, 2, 3)
    ]

    def start(copies):
        for copy in copies:
            copy.start()

    def arrive(copies):
        for copy in copies:
            copy.wait_recv()

    counts = {"gather": 0, "reduce": 0, "exchange": 0}

    def gather_apply(value, weight, nx, beside=None):
        at = counts["gather"]
        counts["gather"] += 1
        sem = at * PER_PHASE
        buf = gathers.at[at]
        gathers[at, z, c] = value

        def across(k):
            own = buf.at[z, c]
            return remote(sem + k, own, own, chip(far_first(k)))

        def source(kk):
            return ring(-far_first(7 - kk))

        def to_core(kk):
            block = buf.at[source(kk), c]
            return remote(sem + 7 + kk, block, block, core)

        to_core(0).start()

        def send(k, carry):
            across(k).start()
            return carry

        lax.fori_loop(0, 7, send, 0)
        acc[pl.ds(0, nx)] = jnp.zeros((nx, ROWS, VEC), F32)
        if beside is not None:
            beside()

        def use(kk):
            to_core(kk).wait_recv()
            zz = source(kk)
            slab = gathers[at, zz].reshape(SLAB, VEC)
            matrix = weight[:, :, lanes(zz)].reshape(nx * ROWS, SLAB)
            got = jnp.dot(matrix, slab, preferred_element_type=F32)
            acc[pl.ds(0, nx)] += got.reshape(nx, ROWS, VEC)

        def step(kk, carry):
            across(7 - kk).wait_recv()
            to_core(kk).start()
            use(kk - 1)
            return carry

        lax.fori_loop(1, 8, step, 0)
        use(7)

        def drain(k, carry):
            across(k).wait_send()
            to_core(k).wait_send()
            return carry

        lax.fori_loop(0, 7, drain, 0)
        to_core(7).wait_send()

    def apply_reduce(weight, nx):
        at = counts["reduce"]
        counts["reduce"] += 1
        sem = (PHASES + at) * PER_PHASE

        def to_core(k):
            return remote(sem + k, dsend.at[k], core_in.at[at, k], core)

        def across(k):
            return remote(sem + 8 + k, rsend.at[k], ring_in.at[at, k], chip(far_first(k)))

        def make(k):
            zz = ring(far_first(k))
            matrix = weight[:, :, lanes(zz)].reshape(nx * ROWS, SLAB)
            right = vals[pl.ds(0, nx)].reshape(nx * ROWS, VEC)
            got = lax.dot_general(
                matrix, right, (((0,), (0,)), ((), ())), preferred_element_type=F32
            )
            part[k] = got.reshape(CORES, ROWS, VEC)
            dsend[k] = part[k, 1 - c].astype(BF)
            to_core(k).start()

        def total(k):
            to_core(k).wait_recv()
            return part[k, c] + core_in[at, k].astype(F32)

        def send(k):
            rsend[k] = total(k).astype(BF)
            across(k).start()

        def first(k, carry):
            make(k)
            return carry

        def step(k, carry):
            make(k)
            send(k - 2)
            return carry

        lax.fori_loop(0, 2, first, 0)
        lax.fori_loop(2, 8, step, 0)
        send(6)

        def collect(i, value):
            k = 6 - i
            across(k).wait_recv()
            return value + ring_in[at, k].astype(F32)

        value = lax.fori_loop(0, 7, collect, total(7))

        def drain(k, carry):
            across(k).wait_send()
            to_core(k).wait_send()
            return carry

        lax.fori_loop(0, 7, drain, 0)
        to_core(7).wait_send()
        return value

    def exchange(distances, fill, width=1):
        at = counts["exchange"]
        counts["exchange"] += 1
        copies = {}
        for d in distances:
            fill(d)
            group = pl.ds(d, width)
            copies[d] = remote(
                2 * PHASES * PER_PHASE + at * 3 + d - 1, esend.at[group], leaf_in.at[at, group],
                peer(d),
            )
            copies[d].start()
        for d in distances:
            copies[d].wait_recv()
        for d in distances:
            copies[d].wait_send()
        return at

    def build_pick(pick, lists, row, first, nx):
        def body(i, carry):
            at = pl.multiple_of(i * SLAB, SLAB)
            listed = lists[pl.ds(row, 1), pl.ds(pl.multiple_of(first * COLS + at, SLAB), SLAB)]
            iota = lax.broadcasted_iota(jnp.int32, (ROWS, SLAB), 0)
            for owner in range(nx):
                hit = iota == listed - (owner * COLS + panel * ROWS)
                pick[owner, :, pl.ds(at, SLAB)] = jnp.where(hit, 1.0, 0.0).astype(BF)
            return carry

        lax.fori_loop(0, RING, body, 0)

    both = (0, 1)
    every = (1, 2, 3)

    def send_acc(d):
        esend[d] = acc[flip(d)].astype(BF)

    def send_acc_pair(d):
        for i in both:
            esend[1 + i] = acc[i].astype(BF)

    start(bulk_w1)
    mine[0].wait()
    gather_apply(rs[0], w0, 1, lambda: build_pick(pick0, sl, leaf, 0, 2))
    solved[0] = acc[0].astype(BF)
    vals[0] = solved[0]
    start(bulk_v1)
    mine[1].wait()
    summed = apply_reduce(v0, 1).astype(BF)
    gather_apply(summed, pick0, 2, lambda: build_pick(pick1, sm, leaf // 2, xi, 4))

    def send_other(d):
        esend[d] = acc[1 - xi].astype(BF)

    at = exchange((1,), send_other)
    carried = acc[xi] + leaf_in[at, 1].astype(F32)
    start(bulk_w2)

    mine[2].wait()
    arrive(bulk_w1)
    gather_apply((rs[1].astype(F32) - carried).astype(BF), w1, 2)
    at = exchange((1,), send_acc_pair, 2)
    for i in both:
        solved[1 + i] = (acc[i] + leaf_in[at, 1 + i].astype(F32)).astype(BF)
        vals[i] = solved[1 + i]
    mine[3].wait()
    arrive(bulk_v1)
    summed = apply_reduce(v1, 2).astype(BF)
    gather_apply(summed, pick1, 4)
    at = exchange(every, send_acc)
    carried = acc[x]
    for d in every:
        carried = carried + leaf_in[at, d].astype(F32)

    mine[4].wait()
    arrive(bulk_w2)
    gather_apply((rs[2].astype(F32) - carried).astype(BF), w2, 4)
    at = exchange(every, send_acc)
    top = acc[x]
    for d in every:
        top = top + leaf_in[at, d].astype(F32)

    def share(value, distances):
        def fill(d):
            esend[d] = value

        at = exchange(distances, fill)
        if len(distances) == 1:
            vals[xi] = value
            vals[1 - xi] = leaf_in[at, 1]
        else:
            vals[x] = value
            for d in distances:
                vals[flip(d)] = leaf_in[at, d]

    share(top.astype(BF), every)
    above = apply_reduce(w2, 4).astype(BF)
    out[2] = above

    share(above, every)
    summed = apply_reduce(pick1, 4).astype(BF)
    gather_apply(summed, v1, 2)
    at = exchange((1,), send_acc_pair, 2)
    for i in both:
        correction = acc[i] + leaf_in[at, 1 + i].astype(F32)
        vals[i] = (solved[1 + i].astype(F32) - correction).astype(BF)
    above = apply_reduce(w1, 2).astype(BF)
    out[1] = above

    share(above, (1,))
    summed = apply_reduce(pick0, 2).astype(BF)
    gather_apply(summed, v0, 1)
    vals[0] = (solved[0].astype(F32) - acc[0]).astype(BF)
    out[0] = apply_reduce(w0, 1).astype(BF)

    for copy in bulk_w1 + bulk_v1 + bulk_w2:
        copy.wait_send()


def on_device(*args):
    vmem = pl.BlockSpec(memory_space=pltpu.VMEM)
    hbm = pl.BlockSpec(memory_space=pl.ANY)
    scratch = [pltpu.VMEM((nx, ROWS, COLS), BF) for nx in (1, 2, 4, 1, 2, 2, 4)]
    scratch += [
        pltpu.VMEM((RING, CORES, ROWS, VEC), F32),
        pltpu.VMEM((4, ROWS, VEC), F32),
        pltpu.VMEM((PHASES, RING, CORES, ROWS, VEC), BF),
        pltpu.VMEM((PHASES, RING, ROWS, VEC), BF),
        pltpu.VMEM((PHASES, RING, ROWS, VEC), BF),
        pltpu.VMEM((EXCHANGES, 4, ROWS, VEC), BF),
        pltpu.VMEM((RING, ROWS, VEC), BF),
        pltpu.VMEM((RING, ROWS, VEC), BF),
        pltpu.VMEM((4, ROWS, VEC), BF),
        pltpu.VMEM((4, ROWS, VEC), BF),
        pltpu.VMEM((3, ROWS, VEC), BF),
        pltpu.SemaphoreType.DMA((5,)),
        pltpu.SemaphoreType.DMA((DATA_SEMS,)),
        pltpu.SemaphoreType.DMA((DATA_SEMS,)),
    ]
    return pl.pallas_call(
        kernel,
        out_shape=jax.ShapeDtypeStruct((3, ROWS, VEC), BF),
        in_specs=[vmem, hbm, hbm, hbm, hbm, hbm, vmem, vmem],
        out_specs=vmem,
        scratch_shapes=scratch,
        compiler_params=pltpu.CompilerParams(
            collective_id=0, has_side_effects=True, vmem_limit_bytes=56 * 1024 * 1024
        ),
    )(*args)


def solution(mesh):
    split = P(("leaf", "panel"), None)
    return jax.shard_map(
        on_device,
        mesh=mesh,
        in_specs=(
            P(None, ("leaf", "panel"), None), split, split, split, split, split, P(), P(),
        ),
        out_specs=P(None, ("leaf", "panel"), None),
        check_vma=False,
    )
```

```python
import jax
import jax.numpy as jnp
from jax import lax
from jax.experimental import pallas as pl
from jax.experimental.pallas import tpu as pltpu
from jax.sharding import PartitionSpec as P

BF = jnp.bfloat16
F32 = jnp.float32
ROWS = 192
VEC = 128
RING = 8
CORES = 2
SLAB = ROWS * CORES
COLS = RING * SLAB
PHASES = 7
EXCHANGES = 8
PER_PHASE = 15
BULK_AT = 2 * PHASES * PER_PHASE + EXCHANGES * 3
DATA_SEMS = BULK_AT + 8
MESH = pl.DeviceIdType.MESH


def kernel(
    rs, il, im, it, ul, um, sl, sm, out,
    w0, w1, w2, v0, v1, pick0, pick1, part, acc, gathers, core_in, ring_in, leaf_in,
    dsend, rsend, esend, vals, solved, wsem, send_sem, recv_sem,
):
    leaf = lax.axis_index("leaf")
    panel = lax.axis_index("panel")
    z = panel // 2
    c = panel % 2
    x = leaf % 4
    xi = leaf % 2
    base = leaf - x

    def ring(off):
        return (z + off + RING) % RING

    def chip(off):
        return (leaf, ring(off) * 2 + c)

    core = (leaf, z * 2 + 1 - c)

    def flip(d):
        if d == 1:
            return x + 1 - 2 * xi
        if d == 2:
            return (x + 2) % 4
        return 3 - x

    def peer(d):
        return (base + flip(d), panel)

    def remote(at, src, dst, device):
        return pltpu.make_async_remote_copy(
            src_ref=src, dst_ref=dst, send_sem=send_sem.at[at], recv_sem=recv_sem.at[at],
            device_id=device, device_id_type=MESH,
        )

    def columns(block):
        return pl.ds(pl.multiple_of(block * COLS, COLS), COLS)

    def lanes(zz):
        return pl.ds(pl.multiple_of(zz * SLAB, SLAB), SLAB)

    mine = [
        pltpu.make_async_copy(il, w0.at[0], wsem.at[0]),
        pltpu.make_async_copy(ul, v0.at[0], wsem.at[1]),
        pltpu.make_async_copy(im.at[:, columns(xi)], w1.at[xi], wsem.at[2]),
        pltpu.make_async_copy(um.at[:, columns(xi)], v1.at[xi], wsem.at[3]),
        pltpu.make_async_copy(it.at[:, columns(x)], w2.at[x], wsem.at[4]),
    ]
    for copy in mine:
        copy.start()

    peers = [chip(off) for off in range(1, RING)] + [core] + [peer(d) for d in (1, 2, 3)]
    barrier = pltpu.get_barrier_semaphore()
    for device in peers:
        pl.semaphore_signal(barrier, inc=1, device_id=device, device_id_type=MESH)
    pl.semaphore_wait(barrier, len(peers))

    class Bulk:
        def __init__(self, at, src, cols, dst, device):
            self.args = at, src, cols, dst, device

        def piece(self, row, rows):
            at, src, cols, dst, device = self.args
            return remote(at, src.at[pl.ds(row, rows), cols], dst.at[pl.ds(row, rows)], device)

        def some(self, first, last):
            for j in range(first, last):
                self.piece(16 * j, 16).start()

        def start(self):
            self.some(0, 12)

        def wait_recv(self):
            self.piece(0, ROWS).wait_recv()

        def wait_send(self):
            self.piece(0, ROWS).wait_send()

    bulk_v1 = Bulk(BULK_AT, um, columns(1 - xi), v1.at[xi], peer(1))
    bulk_w1 = Bulk(BULK_AT + 1, im, columns(1 - xi), w1.at[xi], peer(1))
    bulk_w2 = {d: Bulk(BULK_AT + 1 + d, it, columns(flip(d)), w2.at[x], peer(d)) for d in (1, 2, 3)}

    def when(condition, action):
        pl.when(condition)(action)

    def start_w2(d):
        when(x > flip(d), bulk_w2[d].start)

    def arrive_w2():
        for d in (1, 2, 3):
            when(x < flip(d), bulk_w2[d].wait_recv)

    def clear_above():
        @pl.when(xi == 1)
        def _():
            w1[0] = jnp.zeros((ROWS, COLS), BF)

        for d in (1, 2, 3):
            @pl.when(x > flip(d))
            def _():
                w2[flip(d)] = jnp.zeros((ROWS, COLS), BF)

    pending = []

    def drain():
        for action in pending:
            action()
        pending.clear()

    def choose(k, table):
        value = table[-1]
        for at in range(len(table) - 2, -1, -1):
            value = jnp.where(k == at, table[at], value)
        return value

    def start(copies):
        for copy in copies:
            copy.start()

    def arrive(copies):
        for copy in copies:
            copy.wait_recv()

    paced = [0]

    def pace():
        n = paced[0]
        if n >= 6:
            return
        paced[0] += 1
        for d in (1, 2, 3):
            @pl.when(x > flip(d))
            def _():
                bulk_w2[d].some(2 * n, 2 * n + 2)

    counts = {"gather": 0, "reduce": 0, "exchange": 0}

    def gather_apply(value, weight, nx, beside=None):
        at = counts["gather"]
        counts["gather"] += 1
        sem = at * PER_PHASE
        gathers[at, z, c] = value

        def block(off):
            return gathers.at[at, ring(off), c]

        def across(k, off, to):
            return remote(sem + k, block(off), block(off), chip(to))

        def source(kk):
            return choose(kk, (0, 6, 2, 7, 1, 5, 3, 4))

        def to_core(kk):
            own = block(source(kk))
            return remote(sem + 7 + kk, own, own, core)

        own = [across(k, 0, to) for k, to in ((0, 2), (1, -2), (2, 1), (3, -1), (6, 4))]
        start(own)
        to_core(0).start()
        pace()
        drain()
        acc[pl.ds(0, nx)] = jnp.zeros((nx, ROWS, VEC), F32)
        if beside is not None:
            beside()

        def use(kk):
            to_core(kk).wait_recv()
            zz = ring(source(kk))
            slab = gathers[at, zz].reshape(SLAB, VEC)
            matrix = weight[:, :, lanes(zz)].reshape(nx * ROWS, SLAB)
            got = jnp.dot(matrix, slab, preferred_element_type=F32)
            acc[pl.ds(0, nx)] += got.reshape(nx, ROWS, VEC)

        def forward(kk):
            return across(3 + kk, source(kk), choose(kk, (0, 1, -1)))

        def step(kk, carry):
            across(kk - 1, source(kk), 1).wait_recv()

            @pl.when(kk < 3)
            def _():
                forward(kk).start()

            to_core(kk).start()
            use(kk - 1)
            return carry

        lax.fori_loop(1, 8, step, 0)
        use(7)

        def finish():
            def body(k, carry):
                across(k, 0, 1).wait_send()
                to_core(k).wait_send()
                return carry

            lax.fori_loop(0, 7, body, 0)
            to_core(7).wait_send()

        pending.append(finish)

    def apply_reduce(weight, nx):
        at = counts["reduce"]
        counts["reduce"] += 1
        sem = (PHASES + at) * PER_PHASE

        def to_core(k):
            return remote(sem + k, dsend.at[at, k], core_in.at[at, k], core)

        def across(k):
            to = choose(k, (1, -1, 4, 1, -1, 2, -2))
            return remote(sem + 8 + k, rsend.at[at, k], ring_in.at[at, k], chip(to))

        def make(k):
            zz = ring(choose(k, (3, 5, 4, 1, 7, 2, 6, 0)))
            matrix = weight[:, :, lanes(zz)].reshape(nx * ROWS, SLAB)
            right = vals[pl.ds(0, nx)].reshape(nx * ROWS, VEC)
            got = lax.dot_general(
                matrix, right, (((0,), (0,)), ((), ())), preferred_element_type=F32
            )
            part[k] = got.reshape(CORES, ROWS, VEC)
            dsend[at, k] = part[k, 1 - c].astype(BF)
            to_core(k).start()

        def total(k):
            to_core(k).wait_recv()
            return part[k, c] + core_in[at, k].astype(F32)

        def arrived(k):
            across(k).wait_recv()
            return ring_in[at, k].astype(F32)

        def send(k, value):
            rsend[at, k] = value.astype(BF)
            across(k).start()

        def first(k, carry):
            make(k)
            return carry

        def step(k, carry):
            make(k)
            send(k - 2, total(k - 2))
            return carry

        lax.fori_loop(0, 2, first, 0)
        lax.fori_loop(2, 7, step, 0)
        make(7)
        for k in (5, 6):
            send(k, total(k) + arrived(k - 5))
        pace()
        drain()
        value = total(7)
        for k in (3, 4, 2, 5, 6):
            value = value + arrived(k)

        def finish():
            def body(k, carry):
                across(k).wait_send()
                to_core(k).wait_send()
                return carry

            lax.fori_loop(0, 7, body, 0)
            to_core(7).wait_send()

        pending.append(finish)
        return value

    def exchange(distances, fill, width=1):
        at = counts["exchange"]
        counts["exchange"] += 1
        copies = []
        for d in distances:
            fill(at, d)
            group = pl.ds(d, width)
            copies.append(remote(
                2 * PHASES * PER_PHASE + at * 3 + d - 1, esend.at[at, group],
                leaf_in.at[at, group], peer(d),
            ))
            copies[-1].start()
        drain()
        arrive(copies)
        pending.extend(copy.wait_send for copy in copies)
        return at

    def build_pick(pick, lists, row, first, nx):
        def body(i, carry):
            at = pl.multiple_of(i * SLAB, SLAB)
            listed = lists[pl.ds(row, 1), pl.ds(pl.multiple_of(first * COLS + at, SLAB), SLAB)]
            iota = lax.broadcasted_iota(jnp.int32, (ROWS, SLAB), 0)
            for owner in range(nx):
                hit = iota == listed - (owner * COLS + panel * ROWS)
                pick[owner, :, pl.ds(at, SLAB)] = jnp.where(hit, 1.0, 0.0).astype(BF)
            return carry

        lax.fori_loop(0, RING, body, 0)

    both = (0, 1)
    every = (1, 2, 3)

    def send_acc(at, d):
        esend[at, d] = acc[flip(d)].astype(BF)

    def send_acc_pair(at, d):
        for i in both:
            esend[at, 1 + i] = acc[i].astype(BF)

    def beside_first():
        when(xi == 1, bulk_w1.start)
        build_pick(pick0, sl, leaf, 0, 2)
        clear_above()
        mine[0].wait()

    gather_apply(rs[0], w0, 1, beside_first)
    solved[0] = acc[0].astype(BF)
    vals[0] = solved[0]
    bulk_v1.start()
    mine[1].wait()
    summed = apply_reduce(v0, 1).astype(BF)
    gather_apply(summed, pick0, 2, lambda: build_pick(pick1, sm, leaf // 2, xi, 4))

    def send_other(at, d):
        esend[at, d] = acc[1 - xi].astype(BF)

    at = exchange((1,), send_other)
    carried = acc[xi] + leaf_in[at, 1].astype(F32)

    mine[2].wait()
    when(xi == 0, bulk_w1.wait_recv)
    gather_apply((rs[1].astype(F32) - carried).astype(BF), w1, 2)
    at = exchange((1,), send_acc_pair, 2)
    for i in both:
        solved[1 + i] = (acc[i] + leaf_in[at, 1 + i].astype(F32)).astype(BF)
        vals[i] = solved[1 + i]
    mine[3].wait()
    bulk_v1.wait_recv()
    summed = apply_reduce(v1, 2).astype(BF)
    gather_apply(summed, pick1, 4)
    at = exchange(every, send_acc)
    carried = acc[x]
    for d in every:
        carried = carried + leaf_in[at, d].astype(F32)

    mine[4].wait()
    arrive_w2()
    gather_apply((rs[2].astype(F32) - carried).astype(BF), w2, 4)
    at = exchange(every, send_acc)
    top = acc[x]
    for d in every:
        top = top + leaf_in[at, d].astype(F32)

    def share(value, distances):
        def fill(at, d):
            esend[at, d] = value

        at = exchange(distances, fill)
        if len(distances) == 1:
            vals[xi] = value
            vals[1 - xi] = leaf_in[at, 1]
        else:
            vals[x] = value
            for d in distances:
                vals[flip(d)] = leaf_in[at, d]

    share(top.astype(BF), every)
    above = apply_reduce(w2, 4).astype(BF)
    out[2] = above

    share(above, every)
    summed = apply_reduce(pick1, 4).astype(BF)
    gather_apply(summed, v1, 2)
    at = exchange((1,), send_acc_pair, 2)
    for i in both:
        correction = acc[i] + leaf_in[at, 1 + i].astype(F32)
        vals[i] = (solved[1 + i].astype(F32) - correction).astype(BF)
    above = apply_reduce(w1, 2).astype(BF)
    out[1] = above

    share(above, (1,))
    summed = apply_reduce(pick0, 2).astype(BF)
    gather_apply(summed, v0, 1)
    vals[0] = (solved[0].astype(F32) - acc[0]).astype(BF)
    out[0] = apply_reduce(w0, 1).astype(BF)

    drain()
    bulk_v1.wait_send()
    when(xi == 1, bulk_w1.wait_send)
    for d in every:
        when(x > flip(d), bulk_w2[d].wait_send)


def on_device(*args):
    vmem = pl.BlockSpec(memory_space=pltpu.VMEM)
    hbm = pl.BlockSpec(memory_space=pl.ANY)
    scratch = [pltpu.VMEM((nx, ROWS, COLS), BF) for nx in (1, 2, 4, 1, 2, 2, 4)]
    scratch += [
        pltpu.VMEM((RING, CORES, ROWS, VEC), F32),
        pltpu.VMEM((4, ROWS, VEC), F32),
        pltpu.VMEM((PHASES, RING, CORES, ROWS, VEC), BF),
        pltpu.VMEM((PHASES, RING, ROWS, VEC), BF),
        pltpu.VMEM((PHASES, RING, ROWS, VEC), BF),
        pltpu.VMEM((EXCHANGES, 4, ROWS, VEC), BF),
        pltpu.VMEM((PHASES, RING, ROWS, VEC), BF),
        pltpu.VMEM((PHASES, RING, ROWS, VEC), BF),
        pltpu.VMEM((EXCHANGES, 4, ROWS, VEC), BF),
        pltpu.VMEM((4, ROWS, VEC), BF),
        pltpu.VMEM((3, ROWS, VEC), BF),
        pltpu.SemaphoreType.DMA((5,)),
        pltpu.SemaphoreType.DMA((DATA_SEMS,)),
        pltpu.SemaphoreType.DMA((DATA_SEMS,)),
    ]
    return pl.pallas_call(
        kernel,
        out_shape=jax.ShapeDtypeStruct((3, ROWS, VEC), BF),
        in_specs=[vmem, hbm, hbm, hbm, hbm, hbm, vmem, vmem],
        out_specs=vmem,
        scratch_shapes=scratch,
        compiler_params=pltpu.CompilerParams(
            collective_id=0, has_side_effects=True, vmem_limit_bytes=56 * 1024 * 1024
        ),
    )(*args)


def solution(mesh):
    split = P(("leaf", "panel"), None)
    return jax.shard_map(
        on_device,
        mesh=mesh,
        in_specs=(
            P(None, ("leaf", "panel"), None), split, split, split, split, split, P(), P(),
        ),
        out_specs=P(None, ("leaf", "panel"), None),
        check_vma=False,
    )
```

```python
import jax
import jax.numpy as jnp
from jax import lax
from jax.experimental import pallas as pl
from jax.experimental.pallas import tpu as pltpu
from jax.sharding import PartitionSpec as P

BF = jnp.bfloat16
F32 = jnp.float32
ROWS = 192
VEC = 128
RING = 8
CORES = 2
SLAB = ROWS * CORES
COLS = RING * SLAB
PHASES = 7
EXCHANGES = 8
PER_PHASE = 15
BULK_AT = 2 * PHASES * PER_PHASE + EXCHANGES * 3
DATA_SEMS = BULK_AT + 8
MESH = pl.DeviceIdType.MESH


def kernel(
    rs, il, im, it, ul, um, sl, sm, out,
    w0, w1, w2, v0, v1, pick0, pick1, part, acc, gathers, core_in, ring_in, leaf_in,
    dsend, rsend, esend, vals, solved, wsem, send_sem, recv_sem,
):
    leaf = lax.axis_index("leaf")
    panel = lax.axis_index("panel")
    z = panel // 2
    c = panel % 2
    x = leaf % 4
    xi = leaf % 2
    base = leaf - x

    def ring(off):
        return (z + off) & (RING - 1)

    def chip(off):
        return (leaf, ring(off) * 2 + c)

    core = (leaf, z * 2 + 1 - c)

    def flip(d):
        if d == 1:
            return x + 1 - 2 * xi
        if d == 2:
            return (x + 2) % 4
        return 3 - x

    def peer(d):
        return (base + flip(d), panel)

    def remote(at, src, dst, device):
        return pltpu.make_async_remote_copy(
            src_ref=src, dst_ref=dst, send_sem=send_sem.at[at], recv_sem=recv_sem.at[at],
            device_id=device, device_id_type=MESH,
        )

    def columns(block):
        return pl.ds(pl.multiple_of(block * COLS, COLS), COLS)

    def lanes(zz):
        return pl.ds(pl.multiple_of(zz * SLAB, SLAB), SLAB)

    mine = [
        pltpu.make_async_copy(il, w0.at[0], wsem.at[0]),
        pltpu.make_async_copy(ul, v0.at[0], wsem.at[1]),
        pltpu.make_async_copy(im.at[:, columns(xi)], w1.at[xi], wsem.at[2]),
        pltpu.make_async_copy(um.at[:, columns(xi)], v1.at[xi], wsem.at[3]),
        pltpu.make_async_copy(it.at[:, columns(x)], w2.at[x], wsem.at[4]),
    ]
    for copy in mine:
        copy.start()

    peers = [chip(off) for off in range(1, RING)] + [core] + [peer(d) for d in (1, 2, 3)]
    barrier = pltpu.get_barrier_semaphore()
    for device in peers:
        pl.semaphore_signal(barrier, inc=1, device_id=device, device_id_type=MESH)
    pl.semaphore_wait(barrier, len(peers))

    class Bulk:
        def __init__(self, at, src, cols, dst, device):
            self.args = at, src, cols, dst, device

        def piece(self, row, rows):
            at, src, cols, dst, device = self.args
            return remote(at, src.at[pl.ds(row, rows), cols], dst.at[pl.ds(row, rows)], device)

        def some(self, first, last):
            for j in range(first, last):
                self.piece(16 * j, 16).start()

        def start(self):
            self.some(0, 12)

        def wait_recv(self):
            self.piece(0, ROWS).wait_recv()

        def wait_send(self):
            self.piece(0, ROWS).wait_send()

    bulk_v1 = Bulk(BULK_AT, um, columns(1 - xi), v1.at[xi], peer(1))
    bulk_w1 = Bulk(BULK_AT + 1, im, columns(1 - xi), w1.at[xi], peer(1))
    bulk_w2 = {d: Bulk(BULK_AT + 1 + d, it, columns(flip(d)), w2.at[x], peer(d)) for d in (1, 2, 3)}

    def when(condition, action):
        pl.when(condition)(action)

    def arrive_w2():
        for d in (1, 2, 3):
            when(x < flip(d), bulk_w2[d].wait_recv)

    def clear_above():
        @pl.when(xi == 1)
        def _():
            w1[0] = jnp.zeros((ROWS, COLS), BF)

        for d in (1, 2, 3):
            @pl.when(x > flip(d))
            def _():
                w2[flip(d)] = jnp.zeros((ROWS, COLS), BF)

    pending = []

    def drain():
        for action in pending:
            action()
        pending.clear()

    def choose(k, table):
        packed = sum((entry % RING) << (3 * at) for at, entry in enumerate(table))
        return (packed >> (3 * k)) & (RING - 1)

    def start(copies):
        for copy in copies:
            copy.start()

    def arrive(copies):
        for copy in copies:
            copy.wait_recv()

    bulk_of = {"w1": [(bulk_w1, xi == 1)], "v1": [(bulk_v1, None)]}
    bulk_of["w2"] = [(bulk_w2[d], x > flip(d)) for d in (1, 2, 3)]
    plan = {'g0': [('w1', 6)], 'r0': [('w1', 6), ('v1', 2)], 'g1': [('v1', 4), ('w2', 1)], 'e0': [('v1', 3), ('w2', 2)], 'g2': [('v1', 3), ('w2', 2)], 'e1': [('w2', 3)], 'r1': [('w2', 2)], 'g3': [('w2', 1)], 'e2': [('w2', 1)]}
    sent = {"w1": 0, "v1": 0, "w2": 0}

    def pace(slot, also=None):
        for key, number in plan.get(slot, ()):
            first = sent[key]
            sent[key] += number
            for bulk, condition in bulk_of[key]:
                if condition is None or also is None:
                    ready = also if condition is None else condition
                else:
                    ready = jnp.logical_and(also, condition)
                if ready is None:
                    bulk.some(first, first + number)
                else:
                    when(ready, lambda bulk=bulk: bulk.some(first, first + number))

    counts = {"gather": 0, "reduce": 0, "exchange": 0}

    def gather_apply(value, weight, nx, beside=None):
        at = counts["gather"]
        counts["gather"] += 1
        sem = at * PER_PHASE
        gathers[at, z, c] = value

        def block(off):
            return gathers.at[at, ring(off), c]

        def across(k, off, to):
            return remote(sem + k, block(off), block(off), chip(to))

        def source(kk):
            return choose(kk, (0, 6, 2, 7, 1, 5, 3, 4))

        def to_core(kk):
            own = block(source(kk))
            return remote(sem + 7 + kk, own, own, core)

        own = [across(k, 0, to) for k, to in ((0, 2), (1, -2), (2, 1), (3, -1), (6, 4))]
        start(own)
        to_core(0).start()
        drain()
        acc[pl.ds(0, nx)] = jnp.zeros((nx, ROWS, VEC), F32)
        if beside is not None:
            beside()

        def use(kk):
            to_core(kk).wait_recv()
            zz = ring(source(kk))
            slab = gathers[at, zz].reshape(SLAB, VEC)
            matrix = weight[:, :, lanes(zz)].reshape(nx * ROWS, SLAB)
            got = jnp.dot(matrix, slab, preferred_element_type=F32)
            acc[pl.ds(0, nx)] += got.reshape(nx, ROWS, VEC)

        def forward(kk):
            return across(3 + kk, source(kk), choose(kk, (0, 1, -1)))

        def step(kk, carry):
            across(kk - 1, source(kk), 1).wait_recv()

            @pl.when(kk < 3)
            def _():
                forward(kk).start()

            pace(f"g{at}", kk == 3)

            to_core(kk).start()
            use(kk - 1)
            return carry

        lax.fori_loop(1, 8, step, 0)
        use(7)

        def finish():
            def body(k, carry):
                across(k, 0, 1).wait_send()
                to_core(k).wait_send()
                return carry

            lax.fori_loop(0, 7, body, 0)
            to_core(7).wait_send()

        pending.append(finish)

    def apply_reduce(weight, nx):
        at = counts["reduce"]
        counts["reduce"] += 1
        sem = (PHASES + at) * PER_PHASE

        def to_core(k):
            return remote(sem + k, dsend.at[at, k], core_in.at[at, k], core)

        def across(k):
            to = choose(k, (1, -1, 4, 1, -1, 2, -2))
            return remote(sem + 8 + k, rsend.at[at, k], ring_in.at[at, k], chip(to))

        def make(k):
            zz = ring(choose(k, (3, 5, 4, 1, 7, 2, 6, 0)))
            matrix = weight[:, :, lanes(zz)].reshape(nx * ROWS, SLAB)
            right = vals[pl.ds(0, nx)].reshape(nx * ROWS, VEC)
            got = lax.dot_general(
                matrix, right, (((0,), (0,)), ((), ())), preferred_element_type=F32
            )
            part[k] = got.reshape(CORES, ROWS, VEC)
            dsend[at, k] = part[k, 1 - c].astype(BF)
            to_core(k).start()

        def total(k):
            to_core(k).wait_recv()
            return part[k, c] + core_in[at, k].astype(F32)

        def arrived(k):
            across(k).wait_recv()
            return ring_in[at, k].astype(F32)

        def send(k, value):
            rsend[at, k] = value.astype(BF)
            across(k).start()

        def first(k, carry):
            make(k)
            return carry

        def step(k, carry):
            make(k)
            send(k - 2, total(k - 2))
            return carry

        lax.fori_loop(0, 2, first, 0)
        lax.fori_loop(2, 7, step, 0)
        make(7)
        for k in (5, 6):
            send(k, total(k) + arrived(k - 5))
        pace(f"r{at}")
        drain()
        value = total(7)
        for k in (3, 4, 2, 5, 6):
            value = value + arrived(k)

        def finish():
            def body(k, carry):
                across(k).wait_send()
                to_core(k).wait_send()
                return carry

            lax.fori_loop(0, 7, body, 0)
            to_core(7).wait_send()

        pending.append(finish)
        return value

    def exchange(distances, fill, width=1):
        at = counts["exchange"]
        counts["exchange"] += 1
        copies = []
        for d in distances:
            fill(at, d)
            group = pl.ds(d, width)
            copies.append(remote(
                2 * PHASES * PER_PHASE + at * 3 + d - 1, esend.at[at, group],
                leaf_in.at[at, group], peer(d),
            ))
            copies[-1].start()
        pace(f"e{at}")
        drain()
        arrive(copies)
        pending.extend(copy.wait_send for copy in copies)
        return at

    def build_pick(pick, lists, row, first, nx):
        def body(i, carry):
            at = pl.multiple_of(i * SLAB, SLAB)
            listed = lists[pl.ds(row, 1), pl.ds(pl.multiple_of(first * COLS + at, SLAB), SLAB)]
            iota = lax.broadcasted_iota(jnp.int32, (ROWS, SLAB), 0)
            for owner in range(nx):
                hit = iota == listed - (owner * COLS + panel * ROWS)
                pick[owner, :, pl.ds(at, SLAB)] = jnp.where(hit, 1.0, 0.0).astype(BF)
            return carry

        lax.fori_loop(0, RING, body, 0)

    both = (0, 1)
    every = (1, 2, 3)

    def send_acc(at, d):
        esend[at, d] = acc[flip(d)].astype(BF)

    def send_acc_pair(at, d):
        for i in both:
            esend[at, 1 + i] = acc[i].astype(BF)

    def beside_first():
        build_pick(pick0, sl, leaf, 0, 2)
        clear_above()
        mine[0].wait()

    gather_apply(rs[0], w0, 1, beside_first)
    solved[0] = acc[0].astype(BF)
    vals[0] = solved[0]
    mine[1].wait()
    summed = apply_reduce(v0, 1).astype(BF)
    gather_apply(summed, pick0, 2, lambda: build_pick(pick1, sm, leaf // 2, xi, 4))

    def send_other(at, d):
        esend[at, d] = acc[1 - xi].astype(BF)

    at = exchange((1,), send_other)
    carried = acc[xi] + leaf_in[at, 1].astype(F32)

    mine[2].wait()
    when(xi == 0, bulk_w1.wait_recv)
    gather_apply((rs[1].astype(F32) - carried).astype(BF), w1, 2)
    at = exchange((1,), send_acc_pair, 2)
    for i in both:
        solved[1 + i] = (acc[i] + leaf_in[at, 1 + i].astype(F32)).astype(BF)
        vals[i] = solved[1 + i]
    mine[3].wait()
    bulk_v1.wait_recv()
    summed = apply_reduce(v1, 2).astype(BF)
    gather_apply(summed, pick1, 4)
    at = exchange(every, send_acc)
    carried = acc[x]
    for d in every:
        carried = carried + leaf_in[at, d].astype(F32)

    mine[4].wait()
    arrive_w2()
    gather_apply((rs[2].astype(F32) - carried).astype(BF), w2, 4)
    at = exchange(every, send_acc)
    top = acc[x]
    for d in every:
        top = top + leaf_in[at, d].astype(F32)

    def share(value, distances):
        def fill(at, d):
            esend[at, d] = value

        at = exchange(distances, fill)
        if len(distances) == 1:
            vals[xi] = value
            vals[1 - xi] = leaf_in[at, 1]
        else:
            vals[x] = value
            for d in distances:
                vals[flip(d)] = leaf_in[at, d]

    share(top.astype(BF), every)
    above = apply_reduce(w2, 4).astype(BF)
    out[2] = above

    share(above, every)
    summed = apply_reduce(pick1, 4).astype(BF)
    gather_apply(summed, v1, 2)
    at = exchange((1,), send_acc_pair, 2)
    for i in both:
        correction = acc[i] + leaf_in[at, 1 + i].astype(F32)
        vals[i] = (solved[1 + i].astype(F32) - correction).astype(BF)
    above = apply_reduce(w1, 2).astype(BF)
    out[1] = above

    share(above, (1,))
    summed = apply_reduce(pick0, 2).astype(BF)
    gather_apply(summed, v0, 1)
    vals[0] = (solved[0].astype(F32) - acc[0]).astype(BF)
    out[0] = apply_reduce(w0, 1).astype(BF)

    drain()
    bulk_v1.wait_send()
    when(xi == 1, bulk_w1.wait_send)
    for d in every:
        when(x > flip(d), bulk_w2[d].wait_send)


def on_device(*args):
    vmem = pl.BlockSpec(memory_space=pltpu.VMEM)
    hbm = pl.BlockSpec(memory_space=pl.ANY)
    scratch = [pltpu.VMEM((nx, ROWS, COLS), BF) for nx in (1, 2, 4, 1, 2, 2, 4)]
    scratch += [
        pltpu.VMEM((RING, CORES, ROWS, VEC), F32),
        pltpu.VMEM((4, ROWS, VEC), F32),
        pltpu.VMEM((PHASES, RING, CORES, ROWS, VEC), BF),
        pltpu.VMEM((PHASES, RING, ROWS, VEC), BF),
        pltpu.VMEM((PHASES, RING, ROWS, VEC), BF),
        pltpu.VMEM((EXCHANGES, 4, ROWS, VEC), BF),
        pltpu.VMEM((PHASES, RING, ROWS, VEC), BF),
        pltpu.VMEM((PHASES, RING, ROWS, VEC), BF),
        pltpu.VMEM((EXCHANGES, 4, ROWS, VEC), BF),
        pltpu.VMEM((4, ROWS, VEC), BF),
        pltpu.VMEM((3, ROWS, VEC), BF),
        pltpu.SemaphoreType.DMA((5,)),
        pltpu.SemaphoreType.DMA((DATA_SEMS,)),
        pltpu.SemaphoreType.DMA((DATA_SEMS,)),
    ]
    return pl.pallas_call(
        kernel,
        out_shape=jax.ShapeDtypeStruct((3, ROWS, VEC), BF),
        in_specs=[vmem, hbm, hbm, hbm, hbm, hbm, vmem, vmem],
        out_specs=vmem,
        scratch_shapes=scratch,
        compiler_params=pltpu.CompilerParams(
            collective_id=0, has_side_effects=True, vmem_limit_bytes=56 * 1024 * 1024
        ),
    )(*args)


def solution(mesh):
    split = P(("leaf", "panel"), None)
    return jax.shard_map(
        on_device,
        mesh=mesh,
        in_specs=(
            P(None, ("leaf", "panel"), None), split, split, split, split, split, P(), P(),
        ),
        out_specs=P(None, ("leaf", "panel"), None),
        check_vma=False,
    )
```

```python
import jax
import jax.numpy as jnp
from jax import lax
from jax.experimental import pallas as pl
from jax.experimental.pallas import tpu as pltpu
from jax.sharding import PartitionSpec as P

BF = jnp.bfloat16
F32 = jnp.float32
ROWS = 192
VEC = 128
RING = 8
CORES = 2
SLAB = ROWS * CORES
COLS = RING * SLAB
PHASES = 7
EXCHANGES = 8
PER_PHASE = 15
BULK_AT = 2 * PHASES * PER_PHASE + EXCHANGES * 3
DATA_SEMS = BULK_AT + 8
MESH = pl.DeviceIdType.MESH


def kernel(
    rs, il, im, it, ul, um, sl, sm, out,
    w0, w1, w2, v0, v1, pick0, pick1, part, acc, gathers, core_in, ring_in, leaf_in,
    dsend, rsend, esend, vals, solved, wsem, send_sem, recv_sem,
):
    leaf = lax.axis_index("leaf")
    panel = lax.axis_index("panel")
    z = panel // 2
    c = panel % 2
    x = leaf % 4
    xi = leaf % 2
    base = leaf - x

    def ring(off):
        return (z + off) & (RING - 1)

    def chip(off):
        return (leaf, ring(off) * 2 + c)

    core = (leaf, z * 2 + 1 - c)

    def flip(d):
        if d == 1:
            return x + 1 - 2 * xi
        if d == 2:
            return (x + 2) % 4
        return 3 - x

    def peer(d):
        return (base + flip(d), panel)

    def remote(at, src, dst, device):
        return pltpu.make_async_remote_copy(
            src_ref=src, dst_ref=dst, send_sem=send_sem.at[at], recv_sem=recv_sem.at[at],
            device_id=device, device_id_type=MESH,
        )

    def columns(block):
        return pl.ds(pl.multiple_of(block * COLS, COLS), COLS)

    def lanes(zz):
        return pl.ds(pl.multiple_of(zz * SLAB, SLAB), SLAB)

    mine = [
        pltpu.make_async_copy(il, w0.at[0], wsem.at[0]),
        pltpu.make_async_copy(ul, v0.at[0], wsem.at[1]),
        pltpu.make_async_copy(im.at[:, columns(xi)], w1.at[xi], wsem.at[2]),
        pltpu.make_async_copy(um.at[:, columns(xi)], v1.at[xi], wsem.at[3]),
        pltpu.make_async_copy(it.at[:, columns(x)], w2.at[x], wsem.at[4]),
    ]
    for copy in mine:
        copy.start()

    peers = [chip(off) for off in range(1, RING)] + [core] + [peer(d) for d in (1, 2, 3)]
    barrier = pltpu.get_barrier_semaphore()
    for device in peers:
        pl.semaphore_signal(barrier, inc=1, device_id=device, device_id_type=MESH)
    pl.semaphore_wait(barrier, len(peers))

    class Bulk:
        def __init__(self, at, src, cols, dst, device):
            self.args = at, src, cols, dst, device

        def piece(self, row, rows):
            at, src, cols, dst, device = self.args
            return remote(at, src.at[pl.ds(row, rows), cols], dst.at[pl.ds(row, rows)], device)

        def some(self, first, last):
            for j in range(first, last):
                self.piece(16 * j, 16).start()

        def start(self):
            self.some(0, 12)

        def wait_recv(self):
            self.piece(0, ROWS).wait_recv()

        def wait_send(self):
            self.piece(0, ROWS).wait_send()

    bulk_v1 = Bulk(BULK_AT, um, columns(1 - xi), v1.at[xi], peer(1))
    bulk_w1 = Bulk(BULK_AT + 1, im, columns(1 - xi), w1.at[xi], peer(1))
    bulk_w2 = {d: Bulk(BULK_AT + 1 + d, it, columns(flip(d)), w2.at[x], peer(d)) for d in (1, 2, 3)}

    def when(condition, action):
        pl.when(condition)(action)

    def arrive_w2():
        for d in (1, 2, 3):
            when(x < flip(d), bulk_w2[d].wait_recv)

    def clear_above():
        @pl.when(xi == 1)
        def _():
            w1[0] = jnp.zeros((ROWS, COLS), BF)

        for d in (1, 2, 3):
            @pl.when(x > flip(d))
            def _():
                w2[flip(d)] = jnp.zeros((ROWS, COLS), BF)

    pending = []

    def drain():
        for action in pending:
            action()
        pending.clear()

    def choose(k, table):
        packed = sum((entry % RING) << (3 * at) for at, entry in enumerate(table))
        return (packed >> (3 * k)) & (RING - 1)

    def start(copies):
        for copy in copies:
            copy.start()

    def arrive(copies):
        for copy in copies:
            copy.wait_recv()

    bulk_of = {"w1": [(bulk_w1, xi == 1)], "v1": [(bulk_v1, None)]}
    bulk_of["w2"] = [(bulk_w2[d], x > flip(d)) for d in (1, 2, 3)]
    plan = {'g0': [('w1', 6)], 'r0': [('w1', 6), ('v1', 2)], 'g1': [('v1', 4), ('w2', 1)], 'e0': [('v1', 3), ('w2', 2)], 'g2': [('v1', 3), ('w2', 2)], 'e1': [('w2', 3)], 'r1': [('w2', 2)], 'g3': [('w2', 1)], 'e2': [('w2', 1)]}
    sent = {"w1": 0, "v1": 0, "w2": 0}

    def pace(slot, also=None):
        for key, number in plan.get(slot, ()):
            first = sent[key]
            sent[key] += number
            for bulk, condition in bulk_of[key]:
                if condition is None or also is None:
                    ready = also if condition is None else condition
                else:
                    ready = jnp.logical_and(also, condition)
                if ready is None:
                    bulk.some(first, first + number)
                else:
                    when(ready, lambda bulk=bulk: bulk.some(first, first + number))

    counts = {"gather": 0, "reduce": 0, "exchange": 0}

    def gather_apply(value, weight, nx, beside=None):
        at = counts["gather"]
        counts["gather"] += 1
        sem = at * PER_PHASE
        gathers[at, z, c] = value

        def block(off):
            return gathers.at[at, ring(off), c]

        def across(k, off, to):
            return remote(sem + k, block(off), block(off), chip(to))

        def source(kk):
            return choose(kk, (0, 6, 2, 7, 1, 5, 3, 4))

        def to_core(kk):
            own = block(source(kk))
            return remote(sem + 7 + kk, own, own, core)

        own = [across(k, 0, to) for k, to in ((0, 2), (1, -2), (2, 1), (3, -1), (6, 4))]
        start(own)
        to_core(0).start()
        drain()
        acc[pl.ds(0, nx)] = jnp.zeros((nx, ROWS, VEC), F32)
        if beside is not None:
            beside()

        def use(kk):
            to_core(kk).wait_recv()
            zz = ring(source(kk))
            slab = gathers[at, zz].reshape(SLAB, VEC)
            matrix = weight[:, :, lanes(zz)].reshape(nx * ROWS, SLAB)
            got = jnp.dot(matrix, slab, preferred_element_type=F32)
            acc[pl.ds(0, nx)] += got.reshape(nx, ROWS, VEC)

        def forward(kk):
            return across(3 + kk, source(kk), choose(kk, (0, 1, -1)))

        def step(kk, carry):
            across(kk - 1, source(kk), 1).wait_recv()

            @pl.when(kk < 3)
            def _():
                forward(kk).start()

            pace(f"g{at}", kk == 2)

            to_core(kk).start()
            use(kk - 1)
            return carry

        lax.fori_loop(1, 8, step, 0)
        use(7)

        def finish():
            def body(k, carry):
                across(k, 0, 1).wait_send()
                to_core(k).wait_send()
                return carry

            lax.fori_loop(0, 7, body, 0)
            to_core(7).wait_send()

        pending.append(finish)

    def apply_reduce(weight, nx):
        at = counts["reduce"]
        counts["reduce"] += 1
        sem = (PHASES + at) * PER_PHASE

        def to_core(k):
            return remote(sem + k, dsend.at[at, k], core_in.at[at, k], core)

        def across(k):
            to = choose(k, (1, -1, 4, 1, -1, 2, -2))
            return remote(sem + 8 + k, rsend.at[at, k], ring_in.at[at, k], chip(to))

        def make(k):
            zz = ring(choose(k, (3, 5, 4, 1, 7, 2, 6, 0)))
            matrix = weight[:, :, lanes(zz)].reshape(nx * ROWS, SLAB)
            right = vals[pl.ds(0, nx)].reshape(nx * ROWS, VEC)
            got = lax.dot_general(
                matrix, right, (((0,), (0,)), ((), ())), preferred_element_type=F32
            )
            part[k] = got.reshape(CORES, ROWS, VEC)
            dsend[at, k] = part[k, 1 - c].astype(BF)
            to_core(k).start()

        def total(k):
            to_core(k).wait_recv()
            return part[k, c] + core_in[at, k].astype(F32)

        def arrived(k):
            across(k).wait_recv()
            return ring_in[at, k].astype(F32)

        def send(k, value):
            rsend[at, k] = value.astype(BF)
            across(k).start()

        def first(k, carry):
            make(k)
            return carry

        def step(k, carry):
            make(k)
            send(k - lag, total(k - lag))
            return carry

        lag = 1 if nx == 4 else 2
        lax.fori_loop(0, lag, first, 0)
        lax.fori_loop(lag, 5 + lag, step, 0)
        lax.fori_loop(5 + lag, 8, first, 0)
        for k in (5, 6):
            send(k, total(k) + arrived(k - 5))
        pace(f"r{at}")
        drain()
        value = total(7)
        for k in (3, 4, 2, 5, 6):
            value = value + arrived(k)

        def finish():
            def body(k, carry):
                across(k).wait_send()
                to_core(k).wait_send()
                return carry

            lax.fori_loop(0, 7, body, 0)
            to_core(7).wait_send()

        pending.append(finish)
        return value

    def exchange(distances, fill, width=1):
        at = counts["exchange"]
        counts["exchange"] += 1
        copies = []
        for d in distances:
            fill(at, d)
            group = pl.ds(d, width)
            copies.append(remote(
                2 * PHASES * PER_PHASE + at * 3 + d - 1, esend.at[at, group],
                leaf_in.at[at, group], peer(d),
            ))
            copies[-1].start()
        pace(f"e{at}")
        drain()
        arrive(copies)
        pending.extend(copy.wait_send for copy in copies)
        return at

    def build_pick(pick, lists, row, first, nx):
        def body(i, carry):
            at = pl.multiple_of(i * SLAB, SLAB)
            listed = lists[pl.ds(row, 1), pl.ds(pl.multiple_of(first * COLS + at, SLAB), SLAB)]
            iota = lax.broadcasted_iota(jnp.int32, (ROWS, SLAB), 0)
            for owner in range(nx):
                hit = iota == listed - (owner * COLS + panel * ROWS)
                pick[owner, :, pl.ds(at, SLAB)] = jnp.where(hit, 1.0, 0.0).astype(BF)
            return carry

        lax.fori_loop(0, RING, body, 0)

    both = (0, 1)
    every = (1, 2, 3)

    def send_acc(at, d):
        esend[at, d] = acc[flip(d)].astype(BF)

    def send_acc_pair(at, d):
        for i in both:
            esend[at, 1 + i] = acc[i].astype(BF)

    def beside_first():
        build_pick(pick0, sl, leaf, 0, 2)
        clear_above()
        mine[0].wait()

    gather_apply(rs[0], w0, 1, beside_first)
    solved[0] = acc[0].astype(BF)
    vals[0] = solved[0]
    mine[1].wait()
    summed = apply_reduce(v0, 1).astype(BF)
    gather_apply(summed, pick0, 2, lambda: build_pick(pick1, sm, leaf // 2, xi, 4))

    def send_other(at, d):
        esend[at, d] = acc[1 - xi].astype(BF)

    at = exchange((1,), send_other)
    carried = acc[xi] + leaf_in[at, 1].astype(F32)

    mine[2].wait()
    when(xi == 0, bulk_w1.wait_recv)
    gather_apply((rs[1].astype(F32) - carried).astype(BF), w1, 2)
    at = exchange((1,), send_acc_pair, 2)
    for i in both:
        solved[1 + i] = (acc[i] + leaf_in[at, 1 + i].astype(F32)).astype(BF)
        vals[i] = solved[1 + i]
    mine[3].wait()
    bulk_v1.wait_recv()
    summed = apply_reduce(v1, 2).astype(BF)
    gather_apply(summed, pick1, 4)
    at = exchange(every, send_acc)
    carried = acc[x]
    for d in every:
        carried = carried + leaf_in[at, d].astype(F32)

    mine[4].wait()
    arrive_w2()
    gather_apply((rs[2].astype(F32) - carried).astype(BF), w2, 4)
    at = exchange(every, send_acc)
    top = acc[x]
    for d in every:
        top = top + leaf_in[at, d].astype(F32)

    def share(value, distances):
        def fill(at, d):
            esend[at, d] = value

        at = exchange(distances, fill)
        if len(distances) == 1:
            vals[xi] = value
            vals[1 - xi] = leaf_in[at, 1]
        else:
            vals[x] = value
            for d in distances:
                vals[flip(d)] = leaf_in[at, d]

    share(top.astype(BF), every)
    above = apply_reduce(w2, 4).astype(BF)
    out[2] = above

    share(above, every)
    summed = apply_reduce(pick1, 4).astype(BF)
    gather_apply(summed, v1, 2)
    at = exchange((1,), send_acc_pair, 2)
    for i in both:
        correction = acc[i] + leaf_in[at, 1 + i].astype(F32)
        vals[i] = (solved[1 + i].astype(F32) - correction).astype(BF)
    above = apply_reduce(w1, 2).astype(BF)
    out[1] = above

    share(above, (1,))
    summed = apply_reduce(pick0, 2).astype(BF)
    gather_apply(summed, v0, 1)
    vals[0] = (solved[0].astype(F32) - acc[0]).astype(BF)
    out[0] = apply_reduce(w0, 1).astype(BF)

    drain()
    bulk_v1.wait_send()
    when(xi == 1, bulk_w1.wait_send)
    for d in every:
        when(x > flip(d), bulk_w2[d].wait_send)


def on_device(*args):
    vmem = pl.BlockSpec(memory_space=pltpu.VMEM)
    hbm = pl.BlockSpec(memory_space=pl.ANY)
    scratch = [pltpu.VMEM((nx, ROWS, COLS), BF) for nx in (1, 2, 4, 1, 2, 2, 4)]
    scratch += [
        pltpu.VMEM((RING, CORES, ROWS, VEC), F32),
        pltpu.VMEM((4, ROWS, VEC), F32),
        pltpu.VMEM((PHASES, RING, CORES, ROWS, VEC), BF),
        pltpu.VMEM((PHASES, RING, ROWS, VEC), BF),
        pltpu.VMEM((PHASES, RING, ROWS, VEC), BF),
        pltpu.VMEM((EXCHANGES, 4, ROWS, VEC), BF),
        pltpu.VMEM((PHASES, RING, ROWS, VEC), BF),
        pltpu.VMEM((PHASES, RING, ROWS, VEC), BF),
        pltpu.VMEM((EXCHANGES, 4, ROWS, VEC), BF),
        pltpu.VMEM((4, ROWS, VEC), BF),
        pltpu.VMEM((3, ROWS, VEC), BF),
        pltpu.SemaphoreType.DMA((5,)),
        pltpu.SemaphoreType.DMA((DATA_SEMS,)),
        pltpu.SemaphoreType.DMA((DATA_SEMS,)),
    ]
    return pl.pallas_call(
        kernel,
        out_shape=jax.ShapeDtypeStruct((3, ROWS, VEC), BF),
        in_specs=[vmem, hbm, hbm, hbm, hbm, hbm, vmem, vmem],
        out_specs=vmem,
        scratch_shapes=scratch,
        compiler_params=pltpu.CompilerParams(
            collective_id=0, has_side_effects=True, vmem_limit_bytes=56 * 1024 * 1024
        ),
    )(*args)


def solution(mesh):
    split = P(("leaf", "panel"), None)
    return jax.shard_map(
        on_device,
        mesh=mesh,
        in_specs=(
            P(None, ("leaf", "panel"), None), split, split, split, split, split, P(), P(),
        ),
        out_specs=P(None, ("leaf", "panel"), None),
        check_vma=False,
    )
```
